32 devices in a mesh: groups: 2 (over y), ctx: 8 (over z, x), chan: 2 (over core).
Axes of the slice: x: 2, y: 2, z: 4, core: 2. Of those that a mesh axis runs over, the one named last changes fastest.
Arguments:
- inputs: bfloat16 [2048, 2048], P(('groups', 'ctx'), 'chan'), parts along dimension 0, may hold values from -0.1875 to 0.1875
- out_grad: bfloat16 [2048, 2048], P(('groups', 'ctx'), 'chan'), parts along dimension 0, may hold values from -6 to 6
- filters: bfloat16 [512, 2048], P(None, 'chan'), may hold values from -0.25 to 0.25
Outputs:
- in_grad: bfloat16 [2048, 2048], P(('groups', 'ctx'), 'chan'), parts along dimension 0
- filter_grad: float32 [1024, 2048], P(('groups', 'ctx'), 'chan'), parts along dimension 0
The draws below stay inside these ranges and needn't reach their ends.
There are 2 independent parts, one for each index of `groups`. The reference program is written for one: setup_inputs(seed, part) draws one part's arguments, and reference() takes and returns one part's arrays. A program takes and returns all parts, laid end to end along the dimension named above; an argument that names none is the same for every part. Nothing has to cross between parts.
All inputs are finite; a program needn't handle non-finite values.
Results may differ from the reference program's by a relative error of at most 0.0085.
Values may be sent and summed in bfloat16 or wider, within the bound.
A program may use at most 64 MiB of HBM per device.

```python
import jax
import jax.numpy as jnp

CH = 2048
LAGS = 512
SEQ = 1024


def steps_of(rng, dims, split, low, top_value):
    factor_of = 1.0
    for position, parts in split:
        draws = jax.random.uniform(jax.random.fold_in(jax.random.fold_in(rng, 6), position), (parts,), jnp.float32, low / len(split), top_value / len(split))
        factor_of = factor_of * jnp.repeat(jnp.exp(draws), dims[position] // parts).reshape((-1,) + (1,) * (len(dims) - 1 - position))
    return factor_of


def scatter_about(stream_key, extent, deviation, bound, shards=(), held_as=jnp.bfloat16):
    loudness = steps_of(stream_key, extent, shards, -0.22, 0.18) if shards else 1.0
    array = jax.random.normal(stream_key, extent, jnp.float32) * deviation * loudness
    return jnp.minimum(jnp.maximum(array, -bound), bound).astype(held_as)


def setup_inputs(seed: int = 0, part: int = 0) -> dict:
    key_of = jax.random.split(jax.random.key(seed), 4)
    own_keys = jax.random.split(jax.random.fold_in(key_of[3], part), 4)
    inputs = scatter_about(own_keys[0], (SEQ, CH), SEQ ** -0.5, 0.1875, ((0, 8), (1, 2)))
    out_grad = scatter_about(own_keys[1], (SEQ, CH), 1.0, 6.0, ((0, 8), (1, 2)))
    filters = scatter_about(key_of[2], (LAGS, CH), LAGS ** -0.5, 0.25, ((1, 2),))
    return dict(inputs=inputs, out_grad=out_grad, filters=filters)


def reference(inputs, out_grad, filters):
    positions = inputs.shape[0]
    period = 2 * positions
    values = inputs.astype(jnp.float32)
    grads = out_grad.astype(jnp.float32)
    taps = filters.astype(jnp.float32)
    spec_in = jnp.fft.rfft(values, n=period, axis=0)
    spec_grad = jnp.fft.rfft(grads, n=period, axis=0)
    spec_taps = jnp.fft.rfft(taps, n=period, axis=0)
    in_grad = jnp.fft.irfft(jnp.conj(spec_taps) * spec_grad, n=period, axis=0)[:positions]
    filter_grad = jnp.fft.irfft(spec_grad * jnp.conj(spec_in), n=period, axis=0)[:filters.shape[0]]
    return in_grad.astype(jnp.bfloat16), filter_grad.astype(jnp.float32)
```

```python
import functools
import math

import jax
import jax.numpy as jnp
import numpy as np
from jax import lax
from jax.experimental import pallas as pl
from jax.experimental.pallas import tpu as pltpu
from jax.sharding import PartitionSpec as P

LANES = 128
CHUNK = 16


def passed_along(value, axis, steps):
    count = lax.axis_size(axis)
    initial, last = (max(0, -steps), min(count, count - steps))
    return lax.ppermute(value, axis, [(source, source + steps) for source in range(initial, last)])


def phase_table(row_ids, col_ids, period):
    return 2.0 * math.pi / period * (row_ids * col_ids % period).astype(jnp.float32)


def split_table(table):
    high_part = table.astype(jnp.bfloat16)
    low_part = (table - high_part.astype(jnp.float32)).astype(jnp.bfloat16)
    return (high_part, low_part)


def forward_apply(parts, data):
    first = jnp.dot(parts[0], data, preferred_element_type=jnp.float32)
    return first + jnp.dot(parts[1], data, preferred_element_type=jnp.float32)


def spectral(table, data):
    return jnp.dot(table, data, precision=lax.Precision.HIGH, preferred_element_type=jnp.float32)


def general_plan(inputs, out_grad, filters):
    tok_len = out_grad.shape[0]
    channels = out_grad.shape[1]
    lag_count = filters.shape[0]
    far_reach = lag_count // tok_len
    period = 2 * tok_len
    freq_count = tok_len + 1
    freq_col = jnp.arange(freq_count, dtype=jnp.int32)[:, None]
    time_row = jnp.arange(tok_len, dtype=jnp.int32)[None, :]
    angle_fwd = phase_table(freq_col, time_row, period)
    forward = split_table(jnp.concatenate([jnp.cos(angle_fwd), -jnp.sin(angle_fwd)], axis=0))
    freq_row = jnp.arange(freq_count, dtype=jnp.int32)[None, :]
    weighting = (
        jnp.where((freq_row == 0) | (freq_row == tok_len), 1.0, 2.0).astype(jnp.float32) / period
    )
    back_rows = (tok_len - jnp.arange(tok_len, dtype=jnp.int32))[:, None]
    angle_back = phase_table(back_rows, freq_row, period)
    inverse_in = jnp.concatenate(
        [weighting * jnp.cos(angle_back), -weighting * jnp.sin(angle_back)], axis=1
    )
    lag_rows = ((jnp.arange(period, dtype=jnp.int32) - tok_len) % period)[:, None]
    angle_lag = phase_table(lag_rows, freq_row, period)
    inverse_lag = jnp.concatenate(
        [weighting * jnp.cos(angle_lag), -weighting * jnp.sin(angle_lag)], axis=1
    )
    parity = jnp.where(jnp.arange(freq_count) % 2 == 0, 1.0, -1.0).astype(jnp.float32)
    parity_both = jnp.concatenate([parity, parity])[:, None]
    received = [out_grad]
    current = out_grad
    for offset in range(far_reach):
        current = passed_along(current, "ctx", -1)
        received.append(current)
    tap_blocks = filters.reshape(far_reach, tok_len, channels)
    tap_spec = jnp.einsum("ft,btc->bfc", forward[0], tap_blocks, preferred_element_type=jnp.float32)
    tap_spec = tap_spec + jnp.einsum(
        "ft,btc->bfc", forward[1], tap_blocks, preferred_element_type=jnp.float32
    )
    input_spec = forward_apply(forward, inputs)
    input_re = input_spec[:freq_count]
    input_im = input_spec[freq_count:]
    accum_re = jnp.zeros((freq_count, channels), jnp.float32)
    accum_im = jnp.zeros((freq_count, channels), jnp.float32)
    lag_parts = []
    for offset in range(far_reach + 1):
        grad_spec = forward_apply(forward, received[offset])
        grad_re = grad_spec[:freq_count]
        grad_im = grad_spec[freq_count:]
        if offset >= 1 and offset < far_reach:
            segment = tap_spec[offset - 1] + parity_both * tap_spec[offset]
        elif offset >= 1:
            segment = tap_spec[offset - 1]
        else:
            segment = parity_both * tap_spec[offset]
        seg_re = segment[:freq_count]
        seg_im = segment[freq_count:]
        accum_re = accum_re + grad_re * seg_re + grad_im * seg_im
        accum_im = accum_im + grad_re * seg_im - grad_im * seg_re
        cross = jnp.concatenate(
            [grad_re * input_re + grad_im * input_im, grad_im * input_re - grad_re * input_im],
            axis=0,
        )
        lag_parts.append(spectral(inverse_lag, cross))
    in_grad = spectral(inverse_in, jnp.concatenate([accum_re, accum_im], axis=0)).astype(
        jnp.bfloat16
    )
    segments = [
        lag_parts[index + 1][:tok_len] + lag_parts[index][tok_len:] for index in range(far_reach)
    ]
    partial_value = jnp.concatenate(segments, axis=0)
    filter_grad = lax.psum_scatter(partial_value, "ctx", scatter_dimension=0, tiled=True)
    return (in_grad, filter_grad)


def table_parts(table):
    high_part = table.astype(jnp.bfloat16)
    low_part = (table - high_part.astype(np.float64)).astype(jnp.bfloat16)
    return np.stack([high_part, low_part])


def transform_tables(block):
    order = np.concatenate([np.arange(0, block, 2), np.arange(1, block, 2)])
    steps = (2 * order + 1)[:, None] * np.arange(block)[None, :] % (4 * block)
    angle = np.pi / (2 * block) * steps
    forward = np.concatenate([np.cos(angle), np.sin(angle)], axis=0)
    return table_parts(forward), table_parts(forward.T / block)


def peer_order(count):
    return sorted(range(1, count), key=lambda step: (abs(2 * step - count), step))


def exchange_kernel(
    count, block,
    in_ref, grad_ref, taps_ref, fwd_hbm, inv_hbm,
    out_ref, lag_ref,
    u_buf, g_buf, tap_buf, fwd, inv, g_spec, u_spec, tap_spec, seg_spec, r_high, r_low, q_high, q_low,
    out_buf, lag_buf, send_sem, recv_sem, local_sem,
):
    me = lax.axis_index("ctx")
    tok_len = in_ref.shape[0]
    width = g_buf.shape[2]
    lag_count = taps_ref.shape[0]
    own_lags = lag_count // count
    per_block = block // tok_len
    blocks = g_buf.shape[0]
    segs = lag_count // block
    order = peer_order(count)

    def cols(index):
        return pl.ds(pl.multiple_of(index * width, LANES), width)

    def place(buf, index):
        rows = pl.ds(pl.multiple_of(lax.rem(index, per_block) * tok_len, tok_len), tok_len)
        return buf.at[lax.div(index, per_block), rows, :]

    my_cols = cols(me)
    local = [
        pltpu.make_async_copy(fwd_hbm, fwd, local_sem.at[0]),
        pltpu.make_async_copy(taps_ref.at[:, my_cols], tap_buf, local_sem.at[1]),
        pltpu.make_async_copy(grad_ref.at[:, my_cols], place(g_buf, me), local_sem.at[2]),
        pltpu.make_async_copy(in_ref.at[:, my_cols], place(u_buf, me), local_sem.at[3]),
        pltpu.make_async_copy(inv_hbm, inv, local_sem.at[4]),
    ]
    barrier = pltpu.get_barrier_semaphore()
    for step in order:
        pl.semaphore_signal(
            barrier, inc=1, device_id={"ctx": lax.rem(me + step, count)},
            device_id_type=pl.DeviceIdType.MESH,
        )
    for copy in local:
        copy.start()
    pl.semaphore_wait(barrier, count - 1)

    def send_all(kind, source, target):
        copies = []
        for step in order:
            peer = lax.rem(me + step, count)
            copies.append(
                pltpu.make_async_remote_copy(
                    src_ref=source(peer),
                    dst_ref=target,
                    send_sem=send_sem.at[kind, step],
                    recv_sem=recv_sem.at[kind, step],
                    device_id={"ctx": peer},
                    device_id_type=pl.DeviceIdType.MESH,
                )
            )
            copies[-1].start()
        return copies

    g_copies = send_all(0, lambda peer: grad_ref.at[:, cols(peer)], place(g_buf, me))
    u_copies = send_all(1, lambda peer: in_ref.at[:, cols(peer)], place(u_buf, me))

    def forward(data):
        first = jnp.dot(fwd[0], data, preferred_element_type=jnp.float32)
        return first + jnp.dot(fwd[1], data, preferred_element_type=jnp.float32)

    def inverse(high, low):
        first = jnp.dot(inv[0], high, preferred_element_type=jnp.float32)
        second = jnp.dot(inv[1], high, preferred_element_type=jnp.float32)
        return first + (second + jnp.dot(inv[0], low, preferred_element_type=jnp.float32))

    def lanes(index):
        return slice(index * width, (index + 1) * width)

    def over_chunks(body):
        half = block // 2 // CHUNK
        for sign, start in ((1.0, 0), (-1.0, half)):
            def step(index, carry, sign=sign):
                row = pl.multiple_of(index * CHUNK, CHUNK)
                body(pl.ds(row, CHUNK), pl.ds(row + block, CHUNK), sign)
                return carry
            lax.fori_loop(start, start + half, step, 0)

    def store_split(high, low, rows, where, value):
        top = value.astype(jnp.bfloat16)
        high[rows, where] = top
        low[rows, where] = (value - top.astype(jnp.float32)).astype(jnp.bfloat16)

    local[0].wait()
    local[1].wait()
    tap_spec[...] = forward(
        jnp.concatenate([tap_buf[s * block:(s + 1) * block, :] for s in range(segs)], axis=1)
    )

    def segment_chunk(re, im, sign):
        for d in range(segs + 1):
            real = imag = 0.0
            if d < segs:
                real, imag = tap_spec[re, lanes(d)], tap_spec[im, lanes(d)]
            if d > 0:
                real = real + sign * tap_spec[im, lanes(d - 1)]
                imag = imag - sign * tap_spec[re, lanes(d - 1)]
            seg_spec[re, lanes(d)] = real
            seg_spec[im, lanes(d)] = imag

    over_chunks(segment_chunk)

    local[2].wait()
    for copy in g_copies:
        copy.wait_recv()
    g_spec[...] = forward(jnp.concatenate([g_buf[b] for b in range(blocks)], axis=1))

    def in_chunk(re, im, sign):
        grads = [(g_spec[re, lanes(b)], g_spec[im, lanes(b)]) for b in range(blocks)]
        taps = [(seg_spec[re, lanes(d)], seg_spec[im, lanes(d)]) for d in range(segs + 1)]
        for b in range(blocks):
            real = imag = 0.0
            for d in range(min(segs + 1, blocks - b)):
                gr, gi = grads[b + d]
                hr, hi = taps[d]
                real = real + (gr * hr + gi * hi)
                imag = imag + (gi * hr - gr * hi)
            store_split(r_high, r_low, re, lanes(b), real)
            store_split(r_high, r_low, im, lanes(b), imag)

    over_chunks(in_chunk)
    local[4].wait()
    result = inverse(r_high[...], r_low[...]).astype(jnp.bfloat16)
    for index in range(count):
        rows = index % per_block * tok_len
        out_buf[index] = result[rows:rows + tok_len, lanes(index // per_block)]
    out_copies = send_all(2, lambda peer: out_buf.at[peer], out_ref.at[:, my_cols])
    own_out = pltpu.make_async_copy(out_buf.at[me], out_ref.at[:, my_cols], local_sem.at[5])
    own_out.start()

    local[3].wait()
    for copy in u_copies:
        copy.wait_recv()
    u_spec[...] = forward(jnp.concatenate([u_buf[b] for b in range(blocks)], axis=1))

    def lag_chunk(re, im, sign):
        grads = [(g_spec[re, lanes(b)], g_spec[im, lanes(b)]) for b in range(blocks)]
        values = [(u_spec[re, lanes(b)], u_spec[im, lanes(b)]) for b in range(blocks)]
        cross = []
        for d in range(segs + 1):
            real = imag = jnp.zeros((CHUNK, width), jnp.float32)
            for b in range(d, blocks):
                gr, gi = grads[b]
                ur, ui = values[b - d]
                real = real + (gr * ur + gi * ui)
                imag = imag + (gi * ur - gr * ui)
            cross.append((real, imag))
        for s in range(segs):
            store_split(q_high, q_low, re, lanes(s), cross[s][0] - sign * cross[s + 1][1])
            store_split(q_high, q_low, im, lanes(s), cross[s][1] + sign * cross[s + 1][0])

    over_chunks(lag_chunk)
    lag_result = inverse(q_high[...], q_low[...]).astype(jnp.bfloat16)
    for index in range(count):
        rows = index * own_lags % block
        lag_buf[index] = lag_result[rows:rows + own_lags, lanes(index * own_lags // block)]
    lag_copies = send_all(3, lambda peer: lag_buf.at[peer], lag_ref.at[:, my_cols])
    own_lag = pltpu.make_async_copy(lag_buf.at[me], lag_ref.at[:, my_cols], local_sem.at[6])
    own_lag.start()

    for copy in g_copies + u_copies:
        copy.wait_send()
    own_out.wait()
    own_lag.wait()
    for copy in out_copies + lag_copies:
        copy.wait()


def block_length(tok_len, count, lag_count):
    block = tok_len
    if count % 2 == 0 and lag_count % (2 * tok_len) == 0:
        block = 2 * tok_len
    return block


def whole_lanes(tok_len, channels, lag_count, count):
    block = block_length(tok_len, count, lag_count)
    return (
        count > 1
        and channels % (count * LANES) == 0
        and tok_len % CHUNK == 0
        and block % (2 * CHUNK) == 0
        and lag_count % block == 0
        and lag_count % (count * CHUNK) == 0
        and block % (lag_count // count) == 0
        and count * tok_len <= 4 * lag_count
    )


def per_device(inputs, out_grad, filters):
    tok_len, channels = out_grad.shape
    lag_count = filters.shape[0]
    count = lax.axis_size("ctx")
    if not whole_lanes(tok_len, channels, lag_count, count):
        return general_plan(inputs, out_grad, filters)
    block = block_length(tok_len, count, lag_count)
    width = channels // count
    blocks = count * tok_len // block
    segs = lag_count // block
    own_lags = lag_count // count
    fwd, inv = transform_tables(block)
    bf16, f32 = jnp.bfloat16, jnp.float32
    anywhere = pl.BlockSpec(memory_space=pl.ANY)
    in_grad, lag_grad = pl.pallas_call(
        functools.partial(exchange_kernel, count, block),
        out_shape=(
            jax.ShapeDtypeStruct((tok_len, channels), bf16),
            jax.ShapeDtypeStruct((own_lags, channels), bf16),
        ),
        in_specs=[anywhere] * 5,
        out_specs=(anywhere, anywhere),
        scratch_shapes=[
            pltpu.VMEM((blocks, block, width), bf16),
            pltpu.VMEM((blocks, block, width), bf16),
            pltpu.VMEM((lag_count, width), bf16),
            pltpu.VMEM(fwd.shape, bf16),
            pltpu.VMEM(inv.shape, bf16),
            pltpu.VMEM((2 * block, blocks * width), f32),
            pltpu.VMEM((2 * block, blocks * width), f32),
            pltpu.VMEM((2 * block, segs * width), f32),
            pltpu.VMEM((2 * block, (segs + 1) * width), f32),
            pltpu.VMEM((2 * block, blocks * width), bf16),
            pltpu.VMEM((2 * block, blocks * width), bf16),
            pltpu.VMEM((2 * block, segs * width), bf16),
            pltpu.VMEM((2 * block, segs * width), bf16),
            pltpu.VMEM((count, tok_len, width), bf16),
            pltpu.VMEM((count, own_lags, width), bf16),
            pltpu.SemaphoreType.DMA((4, count)),
            pltpu.SemaphoreType.DMA((4, count)),
            pltpu.SemaphoreType.DMA((7,)),
        ],
        compiler_params=pltpu.CompilerParams(collective_id=0, has_side_effects=True),
    )(inputs, out_grad, filters, jnp.asarray(fwd), jnp.asarray(inv))
    return in_grad, lag_grad.astype(f32)


def solution(mesh):
    return jax.shard_map(
        per_device,
        mesh=mesh,
        in_specs=(P(("groups", "ctx"), "chan"), P(("groups", "ctx"), "chan"), P(None, "chan")),
        out_specs=(P(("groups", "ctx"), "chan"), P(("groups", "ctx"), "chan")),
        check_vma=False,
    )
```

```python
import functools
import math

import jax
import jax.numpy as jnp
import numpy as np
from jax import lax
from jax.experimental import pallas as pl
from jax.experimental.pallas import tpu as pltpu
from jax.sharding import PartitionSpec as P

LANES = 128
CHUNK = 16


def passed_along(value, axis, steps):
    count = lax.axis_size(axis)
    initial, last = (max(0, -steps), min(count, count - steps))
    return lax.ppermute(value, axis, [(source, source + steps) for source in range(initial, last)])


def phase_table(row_ids, col_ids, period):
    return 2.0 * math.pi / period * (row_ids * col_ids % period).astype(jnp.float32)


def split_table(table):
    high_part = table.astype(jnp.bfloat16)
    low_part = (table - high_part.astype(jnp.float32)).astype(jnp.bfloat16)
    return (high_part, low_part)


def forward_apply(parts, data):
    first = jnp.dot(parts[0], data, preferred_element_type=jnp.float32)
    return first + jnp.dot(parts[1], data, preferred_element_type=jnp.float32)


def spectral(table, data):
    return jnp.dot(table, data, precision=lax.Precision.HIGH, preferred_element_type=jnp.float32)


def general_plan(inputs, out_grad, filters):
    tok_len = out_grad.shape[0]
    channels = out_grad.shape[1]
    lag_count = filters.shape[0]
    far_reach = lag_count // tok_len
    period = 2 * tok_len
    freq_count = tok_len + 1
    freq_col = jnp.arange(freq_count, dtype=jnp.int32)[:, None]
    time_row = jnp.arange(tok_len, dtype=jnp.int32)[None, :]
    angle_fwd = phase_table(freq_col, time_row, period)
    forward = split_table(jnp.concatenate([jnp.cos(angle_fwd), -jnp.sin(angle_fwd)], axis=0))
    freq_row = jnp.arange(freq_count, dtype=jnp.int32)[None, :]
    weighting = (
        jnp.where((freq_row == 0) | (freq_row == tok_len), 1.0, 2.0).astype(jnp.float32) / period
    )
    back_rows = (tok_len - jnp.arange(tok_len, dtype=jnp.int32))[:, None]
    angle_back = phase_table(back_rows, freq_row, period)
    inverse_in = jnp.concatenate(
        [weighting * jnp.cos(angle_back), -weighting * jnp.sin(angle_back)], axis=1
    )
    lag_rows = ((jnp.arange(period, dtype=jnp.int32) - tok_len) % period)[:, None]
    angle_lag = phase_table(lag_rows, freq_row, period)
    inverse_lag = jnp.concatenate(
        [weighting * jnp.cos(angle_lag), -weighting * jnp.sin(angle_lag)], axis=1
    )
    parity = jnp.where(jnp.arange(freq_count) % 2 == 0, 1.0, -1.0).astype(jnp.float32)
    parity_both = jnp.concatenate([parity, parity])[:, None]
    received = [out_grad]
    current = out_grad
    for offset in range(far_reach):
        current = passed_along(current, "ctx", -1)
        received.append(current)
    tap_blocks = filters.reshape(far_reach, tok_len, channels)
    tap_spec = jnp.einsum("ft,btc->bfc", forward[0], tap_blocks, preferred_element_type=jnp.float32)
    tap_spec = tap_spec + jnp.einsum(
        "ft,btc->bfc", forward[1], tap_blocks, preferred_element_type=jnp.float32
    )
    input_spec = forward_apply(forward, inputs)
    input_re = input_spec[:freq_count]
    input_im = input_spec[freq_count:]
    accum_re = jnp.zeros((freq_count, channels), jnp.float32)
    accum_im = jnp.zeros((freq_count, channels), jnp.float32)
    lag_parts = []
    for offset in range(far_reach + 1):
        grad_spec = forward_apply(forward, received[offset])
        grad_re = grad_spec[:freq_count]
        grad_im = grad_spec[freq_count:]
        if offset >= 1 and offset < far_reach:
            segment = tap_spec[offset - 1] + parity_both * tap_spec[offset]
        elif offset >= 1:
            segment = tap_spec[offset - 1]
        else:
            segment = parity_both * tap_spec[offset]
        seg_re = segment[:freq_count]
        seg_im = segment[freq_count:]
        accum_re = accum_re + grad_re * seg_re + grad_im * seg_im
        accum_im = accum_im + grad_re * seg_im - grad_im * seg_re
        cross = jnp.concatenate(
            [grad_re * input_re + grad_im * input_im, grad_im * input_re - grad_re * input_im],
            axis=0,
        )
        lag_parts.append(spectral(inverse_lag, cross))
    in_grad = spectral(inverse_in, jnp.concatenate([accum_re, accum_im], axis=0)).astype(
        jnp.bfloat16
    )
    segments = [
        lag_parts[index + 1][:tok_len] + lag_parts[index][tok_len:] for index in range(far_reach)
    ]
    partial_value = jnp.concatenate(segments, axis=0)
    filter_grad = lax.psum_scatter(partial_value, "ctx", scatter_dimension=0, tiled=True)
    return (in_grad, filter_grad)


def table_parts(table):
    high_part = table.astype(jnp.bfloat16)
    low_part = (table - high_part.astype(np.float64)).astype(jnp.bfloat16)
    return np.stack([high_part, low_part])


def transform_tables(block):
    order = np.concatenate([np.arange(0, block, 2), np.arange(1, block, 2)])
    steps = (2 * order + 1)[:, None] * np.arange(block)[None, :] % (4 * block)
    angle = np.pi / (2 * block) * steps
    forward = np.concatenate([np.cos(angle), np.sin(angle)], axis=0)
    return table_parts(forward), table_parts(forward.T / block)


def peer_order(count):
    return sorted(range(1, count), key=lambda step: (-abs(2 * step - count), step))


def exchange_kernel(
    count, block,
    in_ref, grad_ref, taps_ref, fwd_hbm, inv_hbm,
    out_ref, lag_ref,
    u_buf, g_buf, tap_buf, fwd, inv, g_spec, u_spec, tap_spec, seg_spec, r_high, r_low, q_high, q_low,
    out_buf, lag_buf, send_sem, recv_sem, local_sem,
):
    me = lax.axis_index("ctx")
    tok_len = in_ref.shape[0]
    width = g_buf.shape[2]
    lag_count = taps_ref.shape[0]
    own_lags = lag_count // count
    per_block = block // tok_len
    blocks = g_buf.shape[0]
    segs = lag_count // block
    order = peer_order(count)

    def cols(index):
        return pl.ds(pl.multiple_of(index * width, LANES), width)

    def place(buf, index):
        rows = pl.ds(pl.multiple_of(lax.rem(index, per_block) * tok_len, tok_len), tok_len)
        return buf.at[lax.div(index, per_block), rows, :]

    my_cols = cols(me)
    local = [
        pltpu.make_async_copy(fwd_hbm, fwd, local_sem.at[0]),
        pltpu.make_async_copy(taps_ref.at[:, my_cols], tap_buf, local_sem.at[1]),
        pltpu.make_async_copy(grad_ref.at[:, my_cols], place(g_buf, me), local_sem.at[2]),
        pltpu.make_async_copy(in_ref.at[:, my_cols], place(u_buf, me), local_sem.at[3]),
        pltpu.make_async_copy(inv_hbm, inv, local_sem.at[4]),
    ]
    barrier = pltpu.get_barrier_semaphore()
    for step in order:
        pl.semaphore_signal(
            barrier, inc=1, device_id={"ctx": lax.rem(me + step, count)},
            device_id_type=pl.DeviceIdType.MESH,
        )
    for copy in local:
        copy.start()
    pl.semaphore_wait(barrier, count - 1)

    def send_all(kind, source, target):
        copies = []
        for step in order:
            peer = lax.rem(me + step, count)
            copies.append(
                pltpu.make_async_remote_copy(
                    src_ref=source(peer),
                    dst_ref=target,
                    send_sem=send_sem.at[kind, step],
                    recv_sem=recv_sem.at[kind, step],
                    device_id={"ctx": peer},
                    device_id_type=pl.DeviceIdType.MESH,
                )
            )
            copies[-1].start()
        return copies

    g_copies = send_all(0, lambda peer: grad_ref.at[:, cols(peer)], place(g_buf, me))
    u_copies = send_all(1, lambda peer: in_ref.at[:, cols(peer)], place(u_buf, me))

    def forward(data):
        first = jnp.dot(fwd[0], data, preferred_element_type=jnp.float32)
        return first + jnp.dot(fwd[1], data, preferred_element_type=jnp.float32)

    def inverse(high, low):
        first = jnp.dot(inv[0], high, preferred_element_type=jnp.float32)
        second = jnp.dot(inv[1], high, preferred_element_type=jnp.float32)
        return first + (second + jnp.dot(inv[0], low, preferred_element_type=jnp.float32))

    def lanes(index):
        return slice(index * width, (index + 1) * width)

    def over_chunks(body):
        half = block // 2 // CHUNK
        for sign, start in ((1.0, 0), (-1.0, half)):
            def step(index, carry, sign=sign):
                row = pl.multiple_of(index * CHUNK, CHUNK)
                body(pl.ds(row, CHUNK), pl.ds(row + block, CHUNK), sign)
                return carry
            lax.fori_loop(start, start + half, step, 0)

    def store_split(high, low, rows, where, value):
        top = value.astype(jnp.bfloat16)
        high[rows, where] = top
        low[rows, where] = (value - top.astype(jnp.float32)).astype(jnp.bfloat16)

    local[0].wait()
    local[1].wait()
    tap_spec[...] = forward(
        jnp.concatenate([tap_buf[s * block:(s + 1) * block, :] for s in range(segs)], axis=1)
    )

    def segment_chunk(re, im, sign):
        for d in range(segs + 1):
            real = imag = 0.0
            if d < segs:
                real, imag = tap_spec[re, lanes(d)], tap_spec[im, lanes(d)]
            if d > 0:
                real = real + sign * tap_spec[im, lanes(d - 1)]
                imag = imag - sign * tap_spec[re, lanes(d - 1)]
            seg_spec[re, lanes(d)] = real
            seg_spec[im, lanes(d)] = imag

    over_chunks(segment_chunk)

    local[2].wait()
    for copy in g_copies:
        copy.wait_recv()
    g_spec[...] = forward(jnp.concatenate([g_buf[b] for b in range(blocks)], axis=1))

    def in_chunk(re, im, sign):
        grads = [(g_spec[re, lanes(b)], g_spec[im, lanes(b)]) for b in range(blocks)]
        taps = [(seg_spec[re, lanes(d)], seg_spec[im, lanes(d)]) for d in range(segs + 1)]
        for b in range(blocks):
            real = imag = 0.0
            for d in range(min(segs + 1, blocks - b)):
                gr, gi = grads[b + d]
                hr, hi = taps[d]
                real = real + (gr * hr + gi * hi)
                imag = imag + (gi * hr - gr * hi)
            store_split(r_high, r_low, re, lanes(b), real)
            store_split(r_high, r_low, im, lanes(b), imag)

    over_chunks(in_chunk)
    local[4].wait()
    result = inverse(r_high[...], r_low[...]).astype(jnp.bfloat16)
    for index in range(count):
        rows = index % per_block * tok_len
        out_buf[index] = result[rows:rows + tok_len, lanes(index // per_block)]
    out_copies = send_all(2, lambda peer: out_buf.at[peer], out_ref.at[:, my_cols])
    own_out = pltpu.make_async_copy(out_buf.at[me], out_ref.at[:, my_cols], local_sem.at[5])
    own_out.start()

    local[3].wait()
    for copy in u_copies:
        copy.wait_recv()
    u_spec[...] = forward(jnp.concatenate([u_buf[b] for b in range(blocks)], axis=1))

    def lag_chunk(re, im, sign):
        grads = [(g_spec[re, lanes(b)], g_spec[im, lanes(b)]) for b in range(blocks)]
        values = [(u_spec[re, lanes(b)], u_spec[im, lanes(b)]) for b in range(blocks)]
        cross = []
        for d in range(segs + 1):
            real = imag = jnp.zeros((CHUNK, width), jnp.float32)
            for b in range(d, blocks):
                gr, gi = grads[b]
                ur, ui = values[b - d]
                real = real + (gr * ur + gi * ui)
                imag = imag + (gi * ur - gr * ui)
            cross.append((real, imag))
        for s in range(segs):
            store_split(q_high, q_low, re, lanes(s), cross[s][0] - sign * cross[s + 1][1])
            store_split(q_high, q_low, im, lanes(s), cross[s][1] + sign * cross[s + 1][0])

    over_chunks(lag_chunk)
    lag_result = inverse(q_high[...], q_low[...]).astype(jnp.bfloat16)
    for index in range(count):
        rows = index * own_lags % block
        lag_buf[index] = lag_result[rows:rows + own_lags, lanes(index * own_lags // block)]
    lag_copies = send_all(3, lambda peer: lag_buf.at[peer], lag_ref.at[:, my_cols])
    own_lag = pltpu.make_async_copy(lag_buf.at[me], lag_ref.at[:, my_cols], local_sem.at[6])
    own_lag.start()

    for copy in g_copies + u_copies:
        copy.wait_send()
    own_out.wait()
    own_lag.wait()
    for copy in out_copies + lag_copies:
        copy.wait()


def finish_kernel(in_ref, lag_ref, in_out, lag_out, lag_wide, sem):
    move = pltpu.make_async_copy(in_ref, in_out, sem.at[0])
    move.start()
    lag_wide[...] = lag_ref[...].astype(lag_wide.dtype)
    store = pltpu.make_async_copy(lag_wide, lag_out, sem.at[1])
    store.start()
    move.wait()
    store.wait()


def block_length(tok_len, count, lag_count):
    block = tok_len
    if count % 2 == 0 and lag_count % (2 * tok_len) == 0:
        block = 2 * tok_len
    return block


def whole_lanes(tok_len, channels, lag_count, count):
    block = block_length(tok_len, count, lag_count)
    return (
        count > 1
        and channels % (count * LANES) == 0
        and tok_len % CHUNK == 0
        and block % (2 * CHUNK) == 0
        and lag_count % block == 0
        and lag_count % (count * CHUNK) == 0
        and block % (lag_count // count) == 0
        and count * tok_len <= 4 * lag_count
    )


def per_device(inputs, out_grad, filters):
    tok_len, channels = out_grad.shape
    lag_count = filters.shape[0]
    count = lax.axis_size("ctx")
    if not whole_lanes(tok_len, channels, lag_count, count):
        return general_plan(inputs, out_grad, filters)
    block = block_length(tok_len, count, lag_count)
    width = channels // count
    blocks = count * tok_len // block
    segs = lag_count // block
    own_lags = lag_count // count
    fwd, inv = transform_tables(block)
    bf16, f32 = jnp.bfloat16, jnp.float32
    anywhere = pl.BlockSpec(memory_space=pl.ANY)
    in_vmem = pl.BlockSpec(memory_space=pltpu.VMEM)
    in_grad, lag_grad = pl.pallas_call(
        functools.partial(exchange_kernel, count, block),
        out_shape=(
            pltpu.VMEM((tok_len, channels), bf16),
            pltpu.VMEM((own_lags, channels), bf16),
        ),
        in_specs=[anywhere] * 5,
        out_specs=(in_vmem, in_vmem),
        scratch_shapes=[
            pltpu.VMEM((blocks, block, width), bf16),
            pltpu.VMEM((blocks, block, width), bf16),
            pltpu.VMEM((lag_count, width), bf16),
            pltpu.VMEM(fwd.shape, bf16),
            pltpu.VMEM(inv.shape, bf16),
            pltpu.VMEM((2 * block, blocks * width), f32),
            pltpu.VMEM((2 * block, blocks * width), f32),
            pltpu.VMEM((2 * block, segs * width), f32),
            pltpu.VMEM((2 * block, (segs + 1) * width), f32),
            pltpu.VMEM((2 * block, blocks * width), bf16),
            pltpu.VMEM((2 * block, blocks * width), bf16),
            pltpu.VMEM((2 * block, segs * width), bf16),
            pltpu.VMEM((2 * block, segs * width), bf16),
            pltpu.VMEM((count, tok_len, width), bf16),
            pltpu.VMEM((count, own_lags, width), bf16),
            pltpu.SemaphoreType.DMA((4, count)),
            pltpu.SemaphoreType.DMA((4, count)),
            pltpu.SemaphoreType.DMA((7,)),
        ],
        compiler_params=pltpu.CompilerParams(collective_id=0, has_side_effects=True),
    )(inputs, out_grad, filters, jnp.asarray(fwd), jnp.asarray(inv))
    return pl.pallas_call(
        finish_kernel,
        out_shape=(
            jax.ShapeDtypeStruct(in_grad.shape, bf16),
            jax.ShapeDtypeStruct(lag_grad.shape, f32),
        ),
        in_specs=[in_vmem, in_vmem],
        out_specs=(anywhere, anywhere),
        scratch_shapes=[
            pltpu.VMEM(lag_grad.shape, f32),
            pltpu.SemaphoreType.DMA((2,)),
        ],
    )(
        pltpu.with_memory_space_constraint(in_grad, pltpu.VMEM),
        pltpu.with_memory_space_constraint(lag_grad, pltpu.VMEM),
    )


def solution(mesh):
    return jax.shard_map(
        per_device,
        mesh=mesh,
        in_specs=(P(("groups", "ctx"), "chan"), P(("groups", "ctx"), "chan"), P(None, "chan")),
        out_specs=(P(("groups", "ctx"), "chan"), P(("groups", "ctx"), "chan")),
        check_vma=False,
    )
```

```python
import functools
import math

import jax
import jax.numpy as jnp
import numpy as np
from jax import lax
from jax.experimental import pallas as pl
from jax.experimental.pallas import tpu as pltpu
from jax.sharding import PartitionSpec as P

LANES = 128
CHUNK = 16


def passed_along(value, axis, steps):
    count = lax.axis_size(axis)
    initial, last = (max(0, -steps), min(count, count - steps))
    return lax.ppermute(value, axis, [(source, source + steps) for source in range(initial, last)])


def phase_table(row_ids, col_ids, period):
    return 2.0 * math.pi / period * (row_ids * col_ids % period).astype(jnp.float32)


def split_table(table):
    high_part = table.astype(jnp.bfloat16)
    low_part = (table - high_part.astype(jnp.float32)).astype(jnp.bfloat16)
    return (high_part, low_part)


def forward_apply(parts, data):
    first = jnp.dot(parts[0], data, preferred_element_type=jnp.float32)
    return first + jnp.dot(parts[1], data, preferred_element_type=jnp.float32)


def spectral(table, data):
    return jnp.dot(table, data, precision=lax.Precision.HIGH, preferred_element_type=jnp.float32)


def general_plan(inputs, out_grad, filters):
    tok_len = out_grad.shape[0]
    channels = out_grad.shape[1]
    lag_count = filters.shape[0]
    far_reach = lag_count // tok_len
    period = 2 * tok_len
    freq_count = tok_len + 1
    freq_col = jnp.arange(freq_count, dtype=jnp.int32)[:, None]
    time_row = jnp.arange(tok_len, dtype=jnp.int32)[None, :]
    angle_fwd = phase_table(freq_col, time_row, period)
    forward = split_table(jnp.concatenate([jnp.cos(angle_fwd), -jnp.sin(angle_fwd)], axis=0))
    freq_row = jnp.arange(freq_count, dtype=jnp.int32)[None, :]
    weighting = (
        jnp.where((freq_row == 0) | (freq_row == tok_len), 1.0, 2.0).astype(jnp.float32) / period
    )
    back_rows = (tok_len - jnp.arange(tok_len, dtype=jnp.int32))[:, None]
    angle_back = phase_table(back_rows, freq_row, period)
    inverse_in = jnp.concatenate(
        [weighting * jnp.cos(angle_back), -weighting * jnp.sin(angle_back)], axis=1
    )
    lag_rows = ((jnp.arange(period, dtype=jnp.int32) - tok_len) % period)[:, None]
    angle_lag = phase_table(lag_rows, freq_row, period)
    inverse_lag = jnp.concatenate(
        [weighting * jnp.cos(angle_lag), -weighting * jnp.sin(angle_lag)], axis=1
    )
    parity = jnp.where(jnp.arange(freq_count) % 2 == 0, 1.0, -1.0).astype(jnp.float32)
    parity_both = jnp.concatenate([parity, parity])[:, None]
    received = [out_grad]
    current = out_grad
    for offset in range(far_reach):
        current = passed_along(current, "ctx", -1)
        received.append(current)
    tap_blocks = filters.reshape(far_reach, tok_len, channels)
    tap_spec = jnp.einsum("ft,btc->bfc", forward[0], tap_blocks, preferred_element_type=jnp.float32)
    tap_spec = tap_spec + jnp.einsum(
        "ft,btc->bfc", forward[1], tap_blocks, preferred_element_type=jnp.float32
    )
    input_spec = forward_apply(forward, inputs)
    input_re = input_spec[:freq_count]
    input_im = input_spec[freq_count:]
    accum_re = jnp.zeros((freq_count, channels), jnp.float32)
    accum_im = jnp.zeros((freq_count, channels), jnp.float32)
    lag_parts = []
    for offset in range(far_reach + 1):
        grad_spec = forward_apply(forward, received[offset])
        grad_re = grad_spec[:freq_count]
        grad_im = grad_spec[freq_count:]
        if offset >= 1 and offset < far_reach:
            segment = tap_spec[offset - 1] + parity_both * tap_spec[offset]
        elif offset >= 1:
            segment = tap_spec[offset - 1]
        else:
            segment = parity_both * tap_spec[offset]
        seg_re = segment[:freq_count]
        seg_im = segment[freq_count:]
        accum_re = accum_re + grad_re * seg_re + grad_im * seg_im
        accum_im = accum_im + grad_re * seg_im - grad_im * seg_re
        cross = jnp.concatenate(
            [grad_re * input_re + grad_im * input_im, grad_im * input_re - grad_re * input_im],
            axis=0,
        )
        lag_parts.append(spectral(inverse_lag, cross))
    in_grad = spectral(inverse_in, jnp.concatenate([accum_re, accum_im], axis=0)).astype(
        jnp.bfloat16
    )
    segments = [
        lag_parts[index + 1][:tok_len] + lag_parts[index][tok_len:] for index in range(far_reach)
    ]
    partial_value = jnp.concatenate(segments, axis=0)
    filter_grad = lax.psum_scatter(partial_value, "ctx", scatter_dimension=0, tiled=True)
    return (in_grad, filter_grad)


def table_parts(table):
    high_part = table.astype(jnp.bfloat16)
    low_part = (table - high_part.astype(np.float64)).astype(jnp.bfloat16)
    return np.stack([high_part, low_part])


def transform_tables(block):
    order = np.concatenate([np.arange(0, block, 2), np.arange(1, block, 2)])
    steps = (2 * order + 1)[:, None] * np.arange(block)[None, :] % (4 * block)
    angle = np.pi / (2 * block) * steps
    forward = np.concatenate([np.cos(angle), np.sin(angle)], axis=0)
    return table_parts(forward), table_parts(forward.T / block)


def peer_order(count):
    return sorted(range(1, count), key=lambda step: (-abs(2 * step - count), step))


def exchange_kernel(
    count, block,
    in_ref, grad_ref, taps_ref, fwd_hbm, inv_hbm,
    out_ref, lag_ref,
    u_buf, g_buf, tap_buf, fwd, inv, g_spec, u_spec, tap_spec, seg_spec, r_high, r_low, q_high, q_low,
    out_buf, lag_buf, send_sem, recv_sem, local_sem,
):
    me = lax.axis_index("ctx")
    tok_len = in_ref.shape[0]
    width = g_buf.shape[2]
    lag_count = taps_ref.shape[0]
    own_lags = lag_count // count
    per_block = block // tok_len
    blocks = g_buf.shape[0]
    segs = lag_count // block
    order = peer_order(count)

    def cols(index):
        return pl.ds(pl.multiple_of(index * width, LANES), width)

    def place(buf, index):
        rows = pl.ds(pl.multiple_of(lax.rem(index, per_block) * tok_len, tok_len), tok_len)
        return buf.at[lax.div(index, per_block), rows, :]

    my_cols = cols(me)
    local = [
        pltpu.make_async_copy(fwd_hbm, fwd, local_sem.at[0]),
        pltpu.make_async_copy(taps_ref.at[:, my_cols], tap_buf, local_sem.at[1]),
        pltpu.make_async_copy(grad_ref.at[:, my_cols], place(g_buf, me), local_sem.at[2]),
        pltpu.make_async_copy(in_ref.at[:, my_cols], place(u_buf, me), local_sem.at[3]),
        pltpu.make_async_copy(inv_hbm, inv, local_sem.at[4]),
    ]
    barrier = pltpu.get_barrier_semaphore()
    for step in order:
        pl.semaphore_signal(
            barrier, inc=1, device_id={"ctx": lax.rem(me + step, count)},
            device_id_type=pl.DeviceIdType.MESH,
        )
    for copy in local:
        copy.start()
    pl.semaphore_wait(barrier, count - 1)

    def send_all(kind, source, target):
        copies = []
        for step in order if kind % 2 == 0 else order[::-1]:
            peer = lax.rem(me + step, count)
            copies.append(
                pltpu.make_async_remote_copy(
                    src_ref=source(peer),
                    dst_ref=target,
                    send_sem=send_sem.at[kind, step],
                    recv_sem=recv_sem.at[kind, step],
                    device_id={"ctx": peer},
                    device_id_type=pl.DeviceIdType.MESH,
                )
            )
            copies[-1].start()
        return copies

    g_copies = send_all(0, lambda peer: grad_ref.at[:, cols(peer)], place(g_buf, me))
    u_copies = send_all(1, lambda peer: in_ref.at[:, cols(peer)], place(u_buf, me))

    def forward(data):
        first = jnp.dot(fwd[0], data, preferred_element_type=jnp.float32)
        return first + jnp.dot(fwd[1], data, preferred_element_type=jnp.float32)

    def inverse(high, low):
        first = jnp.dot(inv[0], high, preferred_element_type=jnp.float32)
        second = jnp.dot(inv[1], high, preferred_element_type=jnp.float32)
        return first + (second + jnp.dot(inv[0], low, preferred_element_type=jnp.float32))

    def lanes(index):
        return slice(index * width, (index + 1) * width)

    def over_chunks(body):
        half = block // 2 // CHUNK
        for sign, start in ((1.0, 0), (-1.0, half)):
            def step(index, carry, sign=sign):
                row = pl.multiple_of(index * CHUNK, CHUNK)
                body(pl.ds(row, CHUNK), pl.ds(row + block, CHUNK), sign)
                return carry
            lax.fori_loop(start, start + half, step, 0)

    def store_split(high, low, rows, where, value):
        top = value.astype(jnp.bfloat16)
        high[rows, where] = top
        low[rows, where] = (value - top.astype(jnp.float32)).astype(jnp.bfloat16)

    local[0].wait()
    local[1].wait()
    tap_spec[...] = forward(
        jnp.concatenate([tap_buf[s * block:(s + 1) * block, :] for s in range(segs)], axis=1)
    )

    def segment_chunk(re, im, sign):
        for d in range(segs + 1):
            real = imag = 0.0
            if d < segs:
                real, imag = tap_spec[re, lanes(d)], tap_spec[im, lanes(d)]
            if d > 0:
                real = real + sign * tap_spec[im, lanes(d - 1)]
                imag = imag - sign * tap_spec[re, lanes(d - 1)]
            seg_spec[re, lanes(d)] = real
            seg_spec[im, lanes(d)] = imag

    over_chunks(segment_chunk)

    local[2].wait()
    for copy in g_copies:
        copy.wait_recv()
    g_spec[...] = forward(jnp.concatenate([g_buf[b] for b in range(blocks)], axis=1))

    def in_chunk(re, im, sign):
        grads = [(g_spec[re, lanes(b)], g_spec[im, lanes(b)]) for b in range(blocks)]
        taps = [(seg_spec[re, lanes(d)], seg_spec[im, lanes(d)]) for d in range(segs + 1)]
        for b in range(blocks):
            real = imag = 0.0
            for d in range(min(segs + 1, blocks - b)):
                gr, gi = grads[b + d]
                hr, hi = taps[d]
                real = real + (gr * hr + gi * hi)
                imag = imag + (gi * hr - gr * hi)
            store_split(r_high, r_low, re, lanes(b), real)
            store_split(r_high, r_low, im, lanes(b), imag)

    over_chunks(in_chunk)
    local[4].wait()
    result = inverse(r_high[...], r_low[...]).astype(jnp.bfloat16)
    for index in range(count):
        rows = index % per_block * tok_len
        out_buf[index] = result[rows:rows + tok_len, lanes(index // per_block)]
    out_copies = send_all(2, lambda peer: out_buf.at[peer], out_ref.at[:, my_cols])
    own_out = pltpu.make_async_copy(out_buf.at[me], out_ref.at[:, my_cols], local_sem.at[5])
    own_out.start()

    local[3].wait()
    for copy in u_copies:
        copy.wait_recv()
    u_spec[...] = forward(jnp.concatenate([u_buf[b] for b in range(blocks)], axis=1))

    def lag_chunk(re, im, sign):
        grads = [(g_spec[re, lanes(b)], g_spec[im, lanes(b)]) for b in range(blocks)]
        values = [(u_spec[re, lanes(b)], u_spec[im, lanes(b)]) for b in range(blocks)]
        cross = []
        for d in range(segs + 1):
            real = imag = jnp.zeros((CHUNK, width), jnp.float32)
            for b in range(d, blocks):
                gr, gi = grads[b]
                ur, ui = values[b - d]
                real = real + (gr * ur + gi * ui)
                imag = imag + (gi * ur - gr * ui)
            cross.append((real, imag))
        for s in range(segs):
            store_split(q_high, q_low, re, lanes(s), cross[s][0] - sign * cross[s + 1][1])
            store_split(q_high, q_low, im, lanes(s), cross[s][1] + sign * cross[s + 1][0])

    over_chunks(lag_chunk)
    lag_result = inverse(q_high[...], q_low[...]).astype(jnp.bfloat16)
    for index in range(count):
        rows = index * own_lags % block
        lag_buf[index] = lag_result[rows:rows + own_lags, lanes(index * own_lags // block)]
    lag_copies = send_all(3, lambda peer: lag_buf.at[peer], lag_ref.at[:, my_cols])
    own_lag = pltpu.make_async_copy(lag_buf.at[me], lag_ref.at[:, my_cols], local_sem.at[6])
    own_lag.start()

    for copy in g_copies + u_copies:
        copy.wait_send()
    own_out.wait()
    own_lag.wait()
    for copy in out_copies + lag_copies:
        copy.wait()


def finish_kernel(in_ref, lag_ref, in_out, lag_out, lag_wide, sem):
    move = pltpu.make_async_copy(in_ref, in_out, sem.at[0])
    move.start()
    lag_wide[...] = lag_ref[...].astype(lag_wide.dtype)
    store = pltpu.make_async_copy(lag_wide, lag_out, sem.at[1])
    store.start()
    move.wait()
    store.wait()


def block_length(tok_len, count, lag_count):
    block = tok_len
    if count % 2 == 0 and lag_count % (2 * tok_len) == 0:
        block = 2 * tok_len
    return block


def whole_lanes(tok_len, channels, lag_count, count):
    block = block_length(tok_len, count, lag_count)
    return (
        count > 1
        and channels % (count * LANES) == 0
        and tok_len % CHUNK == 0
        and block % (2 * CHUNK) == 0
        and lag_count % block == 0
        and lag_count % (count * CHUNK) == 0
        and block % (lag_count // count) == 0
        and count * tok_len <= 4 * lag_count
    )


def per_device(inputs, out_grad, filters):
    tok_len, channels = out_grad.shape
    lag_count = filters.shape[0]
    count = lax.axis_size("ctx")
    if not whole_lanes(tok_len, channels, lag_count, count):
        return general_plan(inputs, out_grad, filters)
    block = block_length(tok_len, count, lag_count)
    width = channels // count
    blocks = count * tok_len // block
    segs = lag_count // block
    own_lags = lag_count // count
    fwd, inv = transform_tables(block)
    bf16, f32 = jnp.bfloat16, jnp.float32
    anywhere = pl.BlockSpec(memory_space=pl.ANY)
    in_vmem = pl.BlockSpec(memory_space=pltpu.VMEM)
    in_grad, lag_grad = pl.pallas_call(
        functools.partial(exchange_kernel, count, block),
        out_shape=(
            pltpu.VMEM((tok_len, channels), bf16),
            pltpu.VMEM((own_lags, channels), bf16),
        ),
        in_specs=[anywhere] * 5,
        out_specs=(in_vmem, in_vmem),
        scratch_shapes=[
            pltpu.VMEM((blocks, block, width), bf16),
            pltpu.VMEM((blocks, block, width), bf16),
            pltpu.VMEM((lag_count, width), bf16),
            pltpu.VMEM(fwd.shape, bf16),
            pltpu.VMEM(inv.shape, bf16),
            pltpu.VMEM((2 * block, blocks * width), f32),
            pltpu.VMEM((2 * block, blocks * width), f32),
            pltpu.VMEM((2 * block, segs * width), f32),
            pltpu.VMEM((2 * block, (segs + 1) * width), f32),
            pltpu.VMEM((2 * block, blocks * width), bf16),
            pltpu.VMEM((2 * block, blocks * width), bf16),
            pltpu.VMEM((2 * block, segs * width), bf16),
            pltpu.VMEM((2 * block, segs * width), bf16),
            pltpu.VMEM((count, tok_len, width), bf16),
            pltpu.VMEM((count, own_lags, width), bf16),
            pltpu.SemaphoreType.DMA((4, count)),
            pltpu.SemaphoreType.DMA((4, count)),
            pltpu.SemaphoreType.DMA((7,)),
        ],
        compiler_params=pltpu.CompilerParams(collective_id=0, has_side_effects=True),
    )(inputs, out_grad, filters, jnp.asarray(fwd), jnp.asarray(inv))
    return pl.pallas_call(
        finish_kernel,
        out_shape=(
            jax.ShapeDtypeStruct(in_grad.shape, bf16),
            jax.ShapeDtypeStruct(lag_grad.shape, f32),
        ),
        in_specs=[in_vmem, in_vmem],
        out_specs=(anywhere, anywhere),
        scratch_shapes=[
            pltpu.VMEM(lag_grad.shape, f32),
            pltpu.SemaphoreType.DMA((2,)),
        ],
    )(
        pltpu.with_memory_space_constraint(in_grad, pltpu.VMEM),
        pltpu.with_memory_space_constraint(lag_grad, pltpu.VMEM),
    )


def solution(mesh):
    return jax.shard_map(
        per_device,
        mesh=mesh,
        in_specs=(P(("groups", "ctx"), "chan"), P(("groups", "ctx"), "chan"), P(None, "chan")),
        out_specs=(P(("groups", "ctx"), "chan"), P(("groups", "ctx"), "chan")),
        check_vma=False,
    )
```
